128 devices in a mesh: sensor: 32 (over z, y, core), rows: 4 (over x).
Axes of the slice: x: 4, y: 4, z: 4, core: 2. Of those that a mesh axis runs over, the one named last changes fastest.
Arguments:
- photon_charge: bfloat16 [128, 128, 3, 32], P(('sensor', 'rows')), may hold values from 20 to 400
- photon_pixel: int32 [128, 128, 32], P(('sensor', 'rows')), may hold values from 0 to 524287
- photon_count: int32 [128, 128], P(('sensor', 'rows')), may hold values from 0 to 32, as said below
- diffusion_kernel: bfloat16 [3, 21, 21], replicated, may hold values from 0.00045204163 to 0.009033203
- fatter_kernel: bfloat16 [21, 21], replicated, may hold values from 4.529953e-05 to 0.00090408325
- crosstalk: bfloat16 [32, 16, 16], replicated, may hold values from -0.125 to 1.1875
Outputs:
- amplifier_images: float32 [32, 16, 4, 64, 512], P(None, None, 'rows', 'sensor')
The draws below stay inside these ranges and needn't reach their ends.
Inputs may be any that keep to these rules, and one draw needn't show every extreme that they name: Slots 0 to photon_count[i, d] - 1 of block (i, d) are live, the others are ignored. At most 2048 live slots in all reach one owner device.
All inputs are finite; a program needn't handle non-finite values.
Results may differ from the reference program's by a relative error of at most 0.0085.
Values may be sent and summed in bfloat16 or wider, within the bound.
A program may use at most 64 MiB of HBM per device.

```python
import math
import jax
import jax.numpy as jnp
from jax import lax

COLS = 4096
AMPS = 16
KSIZE = 21
DEPTHS = 3
READ_ROWS = 64
CAP = 32
SEGW = 512
BANDS = 4
SENSORS = 32
IMG_ROWS = 512
DEVICES = 128


def draw_photon_count(key, part):
    background = jax.random.randint(jax.random.fold_in(key, 11), (DEVICES, DEVICES), CAP // 8, 3 * CAP // 8 + 1)
    bright_owner = jax.random.randint(jax.random.fold_in(key, 12), (), 0, DEVICES)
    shuffled = jax.random.permutation(jax.random.fold_in(key, 13), DEVICES)
    senders = jnp.where(shuffled < DEVICES // 2, CAP, 0)
    owner_ids = jnp.arange(DEVICES)
    return jnp.where(owner_ids[None, :] == bright_owner, senders[:, None], background).astype(jnp.int32)


def draw_crosstalk(key, part):
    identity = jnp.eye(AMPS, dtype=jnp.float32)[None]
    spread_off = jax.random.uniform(jax.random.fold_in(key, 21), (SENSORS, AMPS, AMPS), jnp.float32, -0.1, 0.1)
    diagonal = jnp.ones((SENSORS, AMPS, AMPS), jnp.float32)
    return (diagonal * identity + spread_off * (1.0 - identity)).astype(jnp.bfloat16)


def plant(array, own_key, least, largest):
    spot = [jax.random.randint(jax.random.fold_in(own_key, axis), (), 0, length) for axis, length in enumerate(array.shape)]
    main_axis = array.shape.index(max(array.shape))
    next_to = spot[:main_axis] + [(spot[main_axis] + 1) % array.shape[main_axis]] + spot[main_axis + 1:]
    return array.at[tuple(spot)].set(least).at[tuple(next_to)].set(largest)


def block_levels(rng, shape, pieces, smallest, high):
    level = 1.0
    for axis_at, parts in pieces:
        steps = jax.random.uniform(jax.random.fold_in(jax.random.fold_in(rng, 6), axis_at), (parts,), jnp.float32, smallest / len(pieces), high / len(pieces))
        level = level * jnp.repeat(jnp.exp(steps), shape[axis_at] // parts).reshape((-1,) + (1,) * (len(shape) - 1 - axis_at))
    return level


def setup_inputs(seed: int = 0) -> dict:
    streams_of = jax.random.split(jax.random.key(seed), 7)
    return {
        "photon_charge": jnp.clip(jnp.exp(math.log(400.0) - 2.9957323 * jax.random.uniform(streams_of[0], (DEVICES, DEVICES, DEPTHS, CAP), jnp.float32) ** block_levels(streams_of[0], (DEVICES, DEVICES, DEPTHS, CAP), ((0, 128),), -0.2, 0.2)), 20.0, 400.0).astype(jnp.bfloat16),
        "photon_pixel": plant(jax.random.randint(streams_of[1], (DEVICES, DEVICES, CAP), 0, 2 * READ_ROWS * COLS), jax.random.fold_in(streams_of[1], 1), 0, (2 * READ_ROWS * COLS) - 1).astype(jnp.int32),
        "photon_count": draw_photon_count(jax.random.fold_in(streams_of[6], 71), 0),
        "diffusion_kernel": jnp.clip(jnp.exp(jax.random.uniform(streams_of[3], (DEPTHS, KSIZE, KSIZE), jnp.float32, math.log(0.00045204163), math.log(0.009033203))), 0.00045204163, 0.009033203).astype(jnp.bfloat16),
        "fatter_kernel": jnp.clip(jnp.exp(jax.random.uniform(streams_of[4], (KSIZE, KSIZE), jnp.float32, math.log(4.5299530029296875e-05), math.log(0.00090408325))), 4.5299530029296875e-05, 0.00090408325).astype(jnp.bfloat16),
        "crosstalk": draw_crosstalk(jax.random.fold_in(streams_of[6], 71), 0),
    }


def correlate(image, kernel):
    half_k = kernel.shape[-1] // 2
    return lax.conv_general_dilated(image, kernel, (1, 1), ((half_k, half_k), (half_k, half_k)), precision=lax.Precision.HIGHEST)


def reference(photon_charge, photon_pixel, photon_count, diffusion_kernel, fatter_kernel, crosstalk):
    slot_ids = jnp.arange(CAP, dtype=jnp.int32)
    live_slot = slot_ids[None, None, :] < photon_count[:, :, None]
    charge = jnp.where(live_slot[:, :, None, :], photon_charge, jnp.zeros((), jnp.bfloat16))
    plane_size = 2 * READ_ROWS * COLS
    diffusion_f = diffusion_kernel.astype(jnp.float32)[None]
    fatter_f = fatter_kernel.astype(jnp.float32)[None, None]

    def one_sensor(sensor):
        charge_sub = lax.dynamic_slice_in_dim(charge, sensor * BANDS, BANDS, 1)
        pixel_sub = lax.dynamic_slice_in_dim(photon_pixel, sensor * BANDS, BANDS, 1)
        band_base = (jnp.arange(BANDS, dtype=jnp.int32) * plane_size)[None, :, None]
        target = (pixel_sub + band_base).reshape(-1)
        charge_rows = jnp.transpose(charge_sub.astype(jnp.float32), (2, 0, 1, 3)).reshape(DEPTHS, -1)
        binned = jax.vmap(lambda values_f: jax.ops.segment_sum(values_f, target, num_segments=BANDS * plane_size))(charge_rows)
        binned = lax.optimization_barrier(binned.astype(jnp.bfloat16)).astype(jnp.float32)
        folded = binned.reshape(DEPTHS, BANDS, 2, READ_ROWS, COLS)
        upper = folded[:, :, 0].reshape(DEPTHS, BANDS * READ_ROWS, COLS)
        bottom = jnp.flip(folded[:, :, 1].reshape(DEPTHS, BANDS * READ_ROWS, COLS), axis=1)
        physical = jnp.concatenate([upper, bottom], axis=1)
        diffused = correlate(physical[None], diffusion_f)[0, 0]
        diffused = lax.optimization_barrier(diffused.astype(jnp.bfloat16)).astype(jnp.float32)
        potential = correlate(diffused[None, None], fatter_f)[0, 0]
        final = diffused * (1.0 - potential)
        half_rows = IMG_ROWS // 2
        readout = jnp.stack([final[:half_rows], jnp.flip(final[half_rows:], axis=0)])
        segments = readout.reshape(2, half_rows, 8, SEGW)
        odd_segment = (jnp.arange(8, dtype=jnp.int32) % 2 == 1)[None, None, :, None]
        segments = jnp.where(odd_segment, jnp.flip(segments, axis=3), segments)
        amplifiers = jnp.transpose(segments, (0, 2, 1, 3)).reshape(AMPS, half_rows, SEGW)
        amplifiers = lax.optimization_barrier(amplifiers.astype(jnp.bfloat16)).astype(jnp.float32)
        matrix = crosstalk[sensor].astype(jnp.float32)
        mixed = jnp.einsum('ij,jrc->irc', matrix, amplifiers, precision=lax.Precision.HIGHEST)
        return mixed.reshape(AMPS, BANDS, READ_ROWS, SEGW)

    return lax.map(one_sensor, jnp.arange(SENSORS, dtype=jnp.int32))
```

```python
import jax
import jax.numpy as jnp
from jax import lax
from jax.experimental import pallas as pl
from jax.experimental.pallas import tpu as pltpu
from jax.sharding import PartitionSpec as P

COLS = 4096
KSIZE = 21
READ_ROWS = 64
HALO = 20
EXT = READ_ROWS + 2 * HALO
TILE_ROWS = 2 * EXT * 4
TRASH = 32 * TILE_ROWS
GROUPS = 6
WIDE = 9 * 128
LIST = 4224
UNROLL = 16


def iota(shape, axis):
    return lax.broadcasted_iota(jnp.int32, shape, axis)


def order_slots(message_ref, out_ref):
    t = message_ref[...].T
    live = t[0:32] > 0.0
    r = (t[96:128].astype(jnp.int32) >> 12) & 63
    first = live & (r < HALO)
    final = live & (r >= READ_ROWS - HALO)
    inner = live & (r >= HALO) & (r < READ_ROWS - HALO)
    below = (iota((32, 32), 1) < iota((32, 32), 0)).astype(jnp.bfloat16)
    rank = jnp.zeros((32, 128), jnp.float32)
    offset = jnp.zeros((1, 128), jnp.float32)
    for member in (first, inner, final, jnp.logical_not(live)):
        ones = jnp.where(member, 1.0, 0.0)
        before = jnp.dot(below, ones.astype(jnp.bfloat16), preferred_element_type=jnp.float32)
        rank = jnp.where(member, before + offset, rank)
        offset = offset + jnp.sum(ones, axis=0, keepdims=True)
    rank = rank.astype(jnp.int32)
    place = iota((32, 128), 0)
    parts = [jnp.zeros((32, 128), jnp.float32)] * 4
    for s in range(32):
        here = place == rank[s : s + 1]
        parts = [p + jnp.where(here, t[c * 32 + s : c * 32 + s + 1], 0.0) for c, p in enumerate(parts)]
    out_ref[...] = jnp.concatenate(parts, axis=0).T


def tables(band_ref, base1_ref, base2_ref, cross_ref, w1_ref, w2_ref, mix_ref):
    band = band_ref[0]
    row8 = iota((8, 128), 0)
    for half in range(2):
        for c1 in range(GROUPS):
            for q in range(6):
                base = jnp.broadcast_to(base1_ref[half, c1 * 6 + q : c1 * 6 + q + 1, :], (8, 128))
                for blk in range(2):
                    rows = []
                    for g in range(6):
                        start = 2 + g * 8 if blk else (10 + g * 8 if g < 4 else (g - 4) * 8)
                        turned = pltpu.roll(base, start, axis=1, stride=1, stride_axis=0)
                        if g == 5:
                            turned = jnp.where(row8 < 2, turned, 0.0)
                        if blk == 0 and g >= 4:
                            turned = jnp.where(band == 0, 0.0, turned)
                        rows.append(turned)
                    w1_ref[half, blk, c1 * 48 : c1 * 48 + 48, q * 128 : q * 128 + 128] = jnp.concatenate(
                        rows, axis=0
                    ).astype(jnp.bfloat16)
            y = iota((8, 128), 1) & 63
            for q in range(2):
                base = jnp.broadcast_to(base2_ref[half, c1 * 2 + q : c1 * 2 + q + 1, :], (8, 128))
                first, second = [], []
                for g in range(4):

                    def turn(by, g=g, base=base):
                        return pltpu.roll(pltpu.roll(base, by, axis=1), g * 8, axis=1, stride=1, stride_axis=0)

                    late = turn(6)
                    second.append(late)
                    first.append(jnp.where(y < 32, turn(118), jnp.where(y < 48, turn(32), late)))
                for blk, rows in ((0, first), (1, second)):
                    w2_ref[half, blk, c1 * 32 : c1 * 32 + 32, q * 128 : q * 128 + 128] = jnp.concatenate(
                        rows, axis=0
                    ).astype(jnp.bfloat16)
    row = iota((256, 128), 0)
    source = iota((256, 128), 1)
    pick = (((row >> 5) * 16 + (row & 15)) == source).astype(jnp.bfloat16)
    column = iota((16, 256), 1)
    amp = ((column >> 2) & 1) * 8 + (column & 3) * 2 + (column >> 7)
    spread = (iota((16, 256), 0) == amp).astype(jnp.bfloat16)
    row = iota((256, 256), 0)
    column = iota((256, 256), 1)
    same = (row >> 4) == ((column >> 3) & 15)
    for g in range(4):
        wide = jnp.dot(
            cross_ref[g * 128 : g * 128 + 128, :], spread, preferred_element_type=jnp.float32
        ).astype(jnp.bfloat16)
        tall = jnp.dot(pick, wide, preferred_element_type=jnp.float32)
        mix_ref[g] = jnp.where(same, tall, 0.0).astype(jnp.bfloat16)


def shifted(tiles, by):
    if by == 0:
        return tiles
    lane = lax.broadcasted_iota(jnp.int32, tiles[0].shape, 1)
    zero = jnp.zeros_like(tiles[0])
    turned = [pltpu.roll(t, (-by) % 128, axis=1) for t in tiles]
    count = len(tiles)
    if by > 0:
        return [
            jnp.where(lane < 128 - by, turned[m], turned[m + 1] if m + 1 < count else zero)
            for m in range(count)
        ]
    return [jnp.where(lane < -by, turned[m - 1] if m else zero, turned[m]) for m in range(count)]


def photons_to_readout(
    band_ref, list_ref, w1_ref, w2_ref, out_ref,
    acc, turned, key_v, key_s, flat, bext, part, dif, fin, sem,
):
    band = band_ref[0]
    for q in range(3):
        t = list_ref[q].T
        turned[q, 0:128, :] = t
        turned[q, 128:256, :] = t
        live = t[0:32] > 0.0
        pixel = t[96:128].astype(jnp.int32)
        u = pixel >> 12
        x = pixel & 4095
        half = u >> 6
        r = u & 63
        tile = (x & 3) * 8 + (x >> 9)
        lane = (x >> 2) & 127
        total = jnp.sum(jnp.where(live, 1, 0), axis=0, keepdims=True)
        heads = jnp.sum(jnp.where(live & (r < HALO), 1, 0), axis=0, keepdims=True)
        tails = jnp.sum(jnp.where(live & (r >= 44), 1, 0), axis=0, keepdims=True)
        last = band == 3
        if q == 0:
            row, first, many = r + HALO, jnp.zeros_like(total), total
        elif q == 1:
            row, first, many = r - 44, total - tails, tails
        else:
            row = jnp.where(last, 147 - r, 84 + r)
            half = jnp.where(last, 1 - half, half)
            first = jnp.where(last, total - tails, 0)
            many = jnp.where(last, tails, heads)
        e = half * EXT + row
        slot = iota((32, 128), 0)
        rot = (lane - iota((32, 128), 1)) & 127
        key_v[q, 0:32, :] = ((tile * EXT + (e >> 1)) << 20) + (((e & 1) * 128 + lane) << 12) + (rot << 5) + slot
        key_v[q, 32:40, :] = jnp.broadcast_to(first, (8, 128))
        key_v[q, 40:48, :] = jnp.broadcast_to(many, (8, 128))
    copy = pltpu.make_async_copy(key_v, key_s, sem)
    copy.start()

    def clear(i, c):
        acc[pl.ds(pl.multiple_of(i * 512, 512), 512), :] = jnp.zeros((512, 128), jnp.float32)
        return c

    lax.fori_loop(0, TRASH // 512, clear, 0)
    acc[TRASH : TRASH + 8, :] = jnp.zeros((8, 128), jnp.float32)
    copy.wait()
    spot = iota((8, 128), 1) + 128 * (iota((8, 128), 0) >> 2)
    for q in range(3):
        step = 8 if q == 0 else 4

        def sender(i, at, q=q, step=step):
            first = key_s[q, 32, i]
            many = key_s[q, 40, i]

            def some(j, c):
                for v in range(step):
                    flat[at + j * step + v] = key_s[q, first + j * step + v, i]
                return c

            some(0, 0)
            lax.fori_loop(1, (many + step - 1) // step, some, 0)
            return at + many

        size = lax.fori_loop(0, 128, sender, 0)

        def finish(i, c, size=size):
            flat[size + i] = jnp.int32(((TRASH // 8) << 20) - (1 << 32))
            return c

        lax.fori_loop(0, 2 * UNROLL, finish, 0)

        def prepare(j, q=q):
            bases, values = [], []
            for v in range(UNROLL):
                key = flat[j * UNROLL + v]
                bases.append(pl.multiple_of(lax.shift_right_logical(key, 20) * 8, 8))
                target = lax.shift_right_logical(key, 12) & 255
                charges = turned[q, pl.ds(key & 31, 8, stride=32), :]
                moved = pltpu.roll(charges, (key >> 5) & 127, axis=1)
                values.append(jnp.where(spot == target, moved, 0.0))
            return tuple(bases), tuple(values)

        def add(j, carry, prepare=prepare):
            bases, values = carry
            following = prepare(j + 1)
            for base, value in zip(bases, values):
                acc[pl.ds(pl.multiple_of(base, 8), 8), :] += value
            return following

        lax.fori_loop(0, (size + UNROLL - 1) // UNROLL, add, prepare(0))

    def diffuse(which, carry):
        half = which >> 1
        blk = which & 1
        start = (half * EXT + blk * 40) * 4
        pad = [jnp.zeros((64, 128), jnp.float32)]
        for p in range(4):
            for k in range(3):
                tiles = pad + [
                    acc[pl.ds((p * 8 + m) * TILE_ROWS + start + k, 64, stride=4), :] for m in range(8)
                ]

                def put(slot, values, k=k):
                    for m in range(9):
                        bext[slot * 192 + k * 64 : slot * 192 + k * 64 + 64, m * 128 : m * 128 + 128] = (
                            values[m].astype(jnp.bfloat16)
                        )

                if p >= 2:
                    put(p - 2, tiles)
                put(p + 2, shifted(tiles, 1))
                if p == 0:
                    put(6, shifted(tiles, 2))
        for t in range(4):
            part[...] = jnp.dot(
                w1_ref[half, blk], bext[t * 192 : (t + 4) * 192, :], preferred_element_type=jnp.float32
            )
            for g in range(3):
                total = gathered(part, 48, g)
                rounded = [jnp.zeros((16, 128), jnp.float32)] + [
                    v.astype(jnp.bfloat16).astype(jnp.float32) for v in total
                ]
                row = pl.multiple_of(blk * 48 + g * 16, 16)

                def keep(slot, values, row=row):
                    for m in range(9):
                        dif[half, slot, pl.ds(row, 16), m * 128 : m * 128 + 128] = values[m].astype(jnp.bfloat16)

                keep(t - 2 if t >= 2 else t + 7, rounded)
                keep(t + 2, shifted(rounded, 1))
                if t == 0:
                    keep(6, shifted(rounded, 2))
        return carry

    lax.fori_loop(0, 4, diffuse, 0)

    def respond(half, carry):
        for blk in range(2):
            for t in range(4):
                pieces = []
                for slot in range(t, t + 4):
                    if blk == 0:
                        pieces.append(dif[half, slot, 0:64, :])
                    else:
                        pieces.append(dif[half, slot, 16:32, :])
                        pieces.append(dif[half, slot, 48:96, :])
                part[0:192, :] = jnp.dot(
                    w2_ref[half, blk], jnp.concatenate(pieces, axis=0), preferred_element_type=jnp.float32
                )
                natural = t - 2 if t >= 2 else t + 7
                for g in range(2):
                    total = gathered(part, 32, g)
                    row = blk * 48 + g * 16
                    for m in range(8):
                        d = dif[half, natural, row : row + 16, m * 128 + 128 : m * 128 + 256].astype(jnp.float32)
                        final = d * (1.0 - total[m])
                        for o in range(2):
                            r0 = blk * 32 + g * 16 + o * 8
                            fin[t, pl.ds(r0 * 16 + (m % 2) * 8 + half * 4 + m // 2, 8, stride=16), :] = final[
                                o * 8 : o * 8 + 8
                            ]
        return carry

    lax.fori_loop(0, 2, respond, 0)

    def pack(d, c):
        base = pl.multiple_of(d * 32, 32)
        for t in range(4):
            a = fin[t, pl.ds(base, 32), :]
            swapped = jnp.concatenate([a[0:8], a[16:24], a[8:16], a[24:32]], axis=0)
            out_ref[d, :, t * 128 : t * 128 + 128] = swapped.astype(jnp.bfloat16)
        return c

    lax.fori_loop(0, 32, pack, 0)


def gathered(part, size, g):
    total = None
    for c1 in range(GROUPS):
        rows = c1 * size + g * 16
        tiles = shifted([part[rows : rows + 16, m * 128 : m * 128 + 128] for m in range(9)], c1 - 3)[1:]
        total = tiles if total is None else [a + b for a, b in zip(total, tiles)]
    return total


def crosstalk_kernel(got_ref, mix_ref, out_ref):
    source = lax.broadcasted_iota(jnp.int32, (512, 512), 0)
    column = lax.broadcasted_iota(jnp.int32, (512, 512), 1)
    place = (source & 127) * 4 + (source >> 7)
    even = (place == column).astype(jnp.bfloat16)
    odd = (511 - place == column).astype(jnp.bfloat16)
    for g in range(4):
        block = got_ref[g * 8 : g * 8 + 8]
        ordered = []
        for parity, order in ((0, even), (1, odd)):
            rows = block[:, parity * 16 : parity * 16 + 16, :].reshape(128, 512)
            ordered.append(jnp.dot(rows, order, preferred_element_type=jnp.float32).astype(jnp.bfloat16))
        mixed = jnp.dot(
            mix_ref[g], jnp.concatenate(ordered, axis=0), preferred_element_type=jnp.float32
        )
        for s in range(8):
            for r in range(2):
                for i0 in range(0, 16, 8):
                    for m in range(4):
                        row = s * 32 + r * 16 + i0
                        start = ((g * 8 + s) * 16 + i0) * 8 + m * 2 + r
                        out_ref[pl.ds(start, 8, stride=8), :] = mixed[row : row + 8, m * 128 : m * 128 + 128]


def shards(photon_charge, photon_pixel, photon_count, diffusion_kernel, fatter_kernel, crosstalk):
    vmem = pl.BlockSpec(memory_space=pltpu.VMEM)
    smem = pl.BlockSpec(memory_space=pltpu.SMEM)
    limit = pltpu.CompilerParams(vmem_limit_bytes=56 * 1024 * 1024)
    counts = photon_count[0]
    live = jnp.arange(32, dtype=jnp.int32)[None, :] < counts[:, None]
    charge = jnp.where(live[:, None, :], photon_charge[0], jnp.zeros((), jnp.bfloat16))
    message = jnp.concatenate(
        [charge.reshape(128, 96).astype(jnp.float32), photon_pixel[0].astype(jnp.float32)], axis=1
    )
    message = pl.pallas_call(
        order_slots,
        out_shape=jax.ShapeDtypeStruct((128, 128), jnp.float32),
        in_specs=[vmem],
        out_specs=vmem,
    )(message)
    own = lax.all_to_all(message, ("sensor", "rows"), split_axis=0, concat_axis=0, tiled=True)
    band = lax.axis_index("rows")

    dk = jnp.pad(diffusion_kernel.astype(jnp.float32), ((0, 0), (0, 43), (0, 3)))
    dk = jnp.stack([dk, jnp.pad(jnp.flip(dk[:, :KSIZE], axis=1), ((0, 0), (0, 43), (0, 0)))])
    base1 = jnp.transpose(dk, (0, 3, 1, 2)).reshape(2, 36, 128)
    fk = jnp.pad(fatter_kernel.astype(jnp.float32), ((0, 43), (0, 3)))
    fk = jnp.stack([fk, jnp.pad(jnp.flip(fk[:KSIZE], axis=0), ((0, 43), (0, 0)))])
    base2 = jnp.transpose(fk, (0, 2, 1)).reshape(2, 12, 128)
    w1, w2, mix = pl.pallas_call(
        tables,
        out_shape=[
            jax.ShapeDtypeStruct((2, 2, 288, 768), jnp.bfloat16),
            jax.ShapeDtypeStruct((2, 2, 192, 256), jnp.bfloat16),
            jax.ShapeDtypeStruct((4, 256, 256), jnp.bfloat16),
        ],
        in_specs=[smem, vmem, vmem, vmem],
        out_specs=[vmem, vmem, vmem],
        cost_estimate=pl.CostEstimate(flops=10**8, bytes_accessed=4 * 10**6, transcendentals=0),
    )(band.reshape(1), base1, base2, crosstalk.reshape(512, 16))

    low = lax.ppermute(own, "rows", [(0, 1), (1, 2), (2, 3)])
    high = lax.ppermute(own, "rows", [(1, 0), (2, 1), (3, 2)])
    high = jnp.where(band == 3, own, high)
    lists = jnp.stack([own, low, high])
    amplifiers = pl.pallas_call(
        photons_to_readout,
        out_shape=jax.ShapeDtypeStruct((32, 32, 512), jnp.bfloat16),
        in_specs=[smem, vmem, vmem, vmem],
        out_specs=vmem,
        scratch_shapes=[
            pltpu.VMEM((TRASH + 8, 128), jnp.float32),
            pltpu.VMEM((3, 256, 128), jnp.float32),
            pltpu.VMEM((3, 48, 128), jnp.int32),
            pltpu.SMEM((3, 48, 128), jnp.int32),
            pltpu.SMEM((LIST,), jnp.int32),
            pltpu.VMEM((7 * 192, WIDE), jnp.bfloat16),
            pltpu.VMEM((288, WIDE), jnp.float32),
            pltpu.VMEM((2, 9, 96, WIDE), jnp.bfloat16),
            pltpu.VMEM((4, 1024, 128), jnp.float32),
            pltpu.SemaphoreType.DMA,
        ],
        compiler_params=limit,
    )(band.reshape(1), lists, w1, w2)

    got = lax.all_to_all(amplifiers, "sensor", split_axis=0, concat_axis=0, tiled=True)
    flat = pl.pallas_call(
        crosstalk_kernel,
        out_shape=jax.ShapeDtypeStruct((4096, 128), jnp.float32),
        in_specs=[vmem, vmem],
        out_specs=vmem,
    )(got, mix)
    flat = flat.reshape(32, 16, 4, 2, 128)
    return jnp.transpose(flat, (0, 1, 3, 2, 4)).reshape(32, 16, 1, 2, 512)


def solution(mesh):
    placed = (
        P(("sensor", "rows"), None, None, None),
        P(("sensor", "rows"), None, None),
        P(("sensor", "rows"), None),
        P(),
        P(),
        P(),
    )
    return jax.shard_map(
        shards,
        mesh=mesh,
        in_specs=placed,
        out_specs=P(None, None, "rows", "sensor", None),
        check_vma=False,
    )
```

```python
import jax
import jax.numpy as jnp
from jax import lax
from jax.experimental import pallas as pl
from jax.experimental.pallas import tpu as pltpu
from jax.sharding import PartitionSpec as P

COLS = 4096
KSIZE = 21
READ_ROWS = 64
HALO = 20
EXT = READ_ROWS + 2 * HALO
TILE_ROWS = 2 * EXT * 4
TRASH = 32 * TILE_ROWS
GROUPS = 6
WIDE = 9 * 128
LIST = 4224
UNROLL = 16


def iota(shape, axis):
    return lax.broadcasted_iota(jnp.int32, shape, axis)


def order_slots(message_ref, out_ref):
    t = message_ref[...].T
    live = t[0:32] > 0.0
    r = (t[96:128].astype(jnp.int32) >> 12) & 63
    first = live & (r < HALO)
    final = live & (r >= READ_ROWS - HALO)
    inner = live & (r >= HALO) & (r < READ_ROWS - HALO)
    below = (iota((32, 32), 1) < iota((32, 32), 0)).astype(jnp.bfloat16)
    rank = jnp.zeros((32, 128), jnp.float32)
    offset = jnp.zeros((1, 128), jnp.float32)
    for member in (first, inner, final, jnp.logical_not(live)):
        ones = jnp.where(member, 1.0, 0.0)
        before = jnp.dot(below, ones.astype(jnp.bfloat16), preferred_element_type=jnp.float32)
        rank = jnp.where(member, before + offset, rank)
        offset = offset + jnp.sum(ones, axis=0, keepdims=True)
    rank = rank.astype(jnp.int32)
    place = iota((32, 128), 0)
    parts = [jnp.zeros((32, 128), jnp.float32)] * 4
    for s in range(32):
        here = place == rank[s : s + 1]
        parts = [p + jnp.where(here, t[c * 32 + s : c * 32 + s + 1], 0.0) for c, p in enumerate(parts)]
    out_ref[...] = jnp.concatenate(parts, axis=0).T


def tables(band_ref, base1_ref, base2_ref, cross_ref, w1_ref, w2_ref, mix_ref):
    band = band_ref[0]
    row8 = iota((8, 128), 0)
    for half in range(2):
        for c1 in range(GROUPS):
            for q in range(6):
                base = jnp.broadcast_to(base1_ref[half, c1 * 6 + q : c1 * 6 + q + 1, :], (8, 128))
                for blk in range(2):
                    rows = []
                    for g in range(6):
                        start = 2 + g * 8 if blk else (10 + g * 8 if g < 4 else (g - 4) * 8)
                        turned = pltpu.roll(base, start, axis=1, stride=1, stride_axis=0)
                        if g == 5:
                            turned = jnp.where(row8 < 2, turned, 0.0)
                        if blk == 0 and g >= 4:
                            turned = jnp.where(band == 0, 0.0, turned)
                        rows.append(turned)
                    w1_ref[half, blk, c1 * 48 : c1 * 48 + 48, q * 128 : q * 128 + 128] = jnp.concatenate(
                        rows, axis=0
                    ).astype(jnp.bfloat16)
            y = iota((8, 128), 1) & 63
            for q in range(2):
                base = jnp.broadcast_to(base2_ref[half, c1 * 2 + q : c1 * 2 + q + 1, :], (8, 128))
                first, second = [], []
                for g in range(4):

                    def turn(by, g=g, base=base):
                        return pltpu.roll(pltpu.roll(base, by, axis=1), g * 8, axis=1, stride=1, stride_axis=0)

                    late = turn(6)
                    second.append(late)
                    first.append(jnp.where(y < 32, turn(118), jnp.where(y < 48, turn(32), late)))
                for blk, rows in ((0, first), (1, second)):
                    w2_ref[half, blk, c1 * 32 : c1 * 32 + 32, q * 128 : q * 128 + 128] = jnp.concatenate(
                        rows, axis=0
                    ).astype(jnp.bfloat16)
    row = iota((256, 128), 0)
    source = iota((256, 128), 1)
    pick = (((row >> 5) * 16 + (row & 15)) == source).astype(jnp.bfloat16)
    column = iota((16, 256), 1)
    amp = ((column >> 2) & 1) * 8 + (column & 3) * 2 + (column >> 7)
    spread = (iota((16, 256), 0) == amp).astype(jnp.bfloat16)
    row = iota((256, 256), 0)
    column = iota((256, 256), 1)
    same = (row >> 4) == ((column >> 3) & 15)
    for g in range(4):
        wide = jnp.dot(
            cross_ref[g * 128 : g * 128 + 128, :], spread, preferred_element_type=jnp.float32
        ).astype(jnp.bfloat16)
        tall = jnp.dot(pick, wide, preferred_element_type=jnp.float32)
        mix_ref[g] = jnp.where(same, tall, 0.0).astype(jnp.bfloat16)


def shifted(tiles, by):
    if by == 0:
        return tiles
    lane = lax.broadcasted_iota(jnp.int32, tiles[0].shape, 1)
    zero = jnp.zeros_like(tiles[0])
    turned = [pltpu.roll(t, (-by) % 128, axis=1) for t in tiles]
    count = len(tiles)
    if by > 0:
        return [
            jnp.where(lane < 128 - by, turned[m], turned[m + 1] if m + 1 < count else zero)
            for m in range(count)
        ]
    return [jnp.where(lane < -by, turned[m - 1] if m else zero, turned[m]) for m in range(count)]


def photons_to_readout(
    band_ref, list_ref, w1_ref, w2_ref, out_ref,
    acc, turned, key_v, key_s, flat, bext, part, dif, fin, sem,
):
    band = band_ref[0]
    for q in range(3):
        t = list_ref[q]
        if q == 1:
            t = jnp.where(band == 0, 0.0, t)
        if q == 2:
            t = jnp.where(band == 3, list_ref[0], t)
        t = t.T
        turned[q, 0:128, :] = t
        turned[q, 128:256, :] = t
        live = t[0:32] > 0.0
        pixel = t[96:128].astype(jnp.int32)
        u = pixel >> 12
        x = pixel & 4095
        half = u >> 6
        r = u & 63
        tile = (x & 3) * 8 + (x >> 9)
        lane = (x >> 2) & 127
        total = jnp.sum(jnp.where(live, 1, 0), axis=0, keepdims=True)
        heads = jnp.sum(jnp.where(live & (r < HALO), 1, 0), axis=0, keepdims=True)
        tails = jnp.sum(jnp.where(live & (r >= 44), 1, 0), axis=0, keepdims=True)
        last = band == 3
        if q == 0:
            row, first, many = r + HALO, jnp.zeros_like(total), total
        elif q == 1:
            row, first, many = r - 44, total - tails, tails
        else:
            row = jnp.where(last, 147 - r, 84 + r)
            half = jnp.where(last, 1 - half, half)
            first = jnp.where(last, total - tails, 0)
            many = jnp.where(last, tails, heads)
        e = half * EXT + row
        slot = iota((32, 128), 0)
        rot = (lane - iota((32, 128), 1)) & 127
        key_v[q, 0:32, :] = ((tile * EXT + (e >> 1)) << 20) + (((e & 1) * 128 + lane) << 12) + (rot << 5) + slot
        key_v[q, 32:40, :] = jnp.broadcast_to(first, (8, 128))
        key_v[q, 40:48, :] = jnp.broadcast_to(many, (8, 128))
    copy = pltpu.make_async_copy(key_v, key_s, sem)
    copy.start()

    def clear(i, c):
        acc[pl.ds(pl.multiple_of(i * 512, 512), 512), :] = jnp.zeros((512, 128), jnp.float32)
        return c

    lax.fori_loop(0, TRASH // 512, clear, 0)
    acc[TRASH : TRASH + 8, :] = jnp.zeros((8, 128), jnp.float32)
    copy.wait()
    spot = iota((8, 128), 1) + 128 * (iota((8, 128), 0) >> 2)
    for q in range(3):
        step = 8 if q == 0 else 4

        def sender(i, at, q=q, step=step):
            first = key_s[q, 32, i]
            many = key_s[q, 40, i]

            def some(j, c):
                for v in range(step):
                    flat[at + j * step + v] = key_s[q, first + j * step + v, i]
                return c

            some(0, 0)
            lax.fori_loop(1, (many + step - 1) // step, some, 0)
            return at + many

        size = lax.fori_loop(0, 128, sender, 0)

        def finish(i, c, size=size):
            flat[size + i] = jnp.int32(((TRASH // 8) << 20) - (1 << 32))
            return c

        lax.fori_loop(0, 2 * UNROLL, finish, 0)

        def prepare(j, q=q):
            bases, values = [], []
            for v in range(UNROLL):
                key = flat[j * UNROLL + v]
                bases.append(pl.multiple_of(lax.shift_right_logical(key, 20) * 8, 8))
                target = lax.shift_right_logical(key, 12) & 255
                charges = turned[q, pl.ds(key & 31, 8, stride=32), :]
                moved = pltpu.roll(charges, (key >> 5) & 127, axis=1)
                values.append(jnp.where(spot == target, moved, 0.0))
            return tuple(bases), tuple(values)

        def add(j, carry, prepare=prepare):
            bases, values = carry
            following = prepare(j + 1)
            for base, value in zip(bases, values):
                acc[pl.ds(pl.multiple_of(base, 8), 8), :] += value
            return following

        lax.fori_loop(0, (size + UNROLL - 1) // UNROLL, add, prepare(0))

    def diffuse(which, carry):
        half = which >> 1
        blk = which & 1
        start = (half * EXT + blk * 40) * 4
        pad = [jnp.zeros((64, 128), jnp.float32)]
        for p in range(4):
            for k in range(3):
                tiles = pad + [
                    acc[pl.ds((p * 8 + m) * TILE_ROWS + start + k, 64, stride=4), :] for m in range(8)
                ]

                def put(slot, values, k=k):
                    for m in range(9):
                        bext[slot * 192 + k * 64 : slot * 192 + k * 64 + 64, m * 128 : m * 128 + 128] = (
                            values[m].astype(jnp.bfloat16)
                        )

                if p >= 2:
                    put(p - 2, tiles)
                put(p + 2, shifted(tiles, 1))
                if p == 0:
                    put(6, shifted(tiles, 2))
        for t in range(4):
            part[...] = jnp.dot(
                w1_ref[half, blk], bext[t * 192 : (t + 4) * 192, :], preferred_element_type=jnp.float32
            )
            for g in range(3):
                total = gathered(part, 48, g)
                rounded = [jnp.zeros((16, 128), jnp.float32)] + [
                    v.astype(jnp.bfloat16).astype(jnp.float32) for v in total
                ]
                row = pl.multiple_of(blk * 48 + g * 16, 16)

                def keep(slot, values, row=row):
                    for m in range(9):
                        dif[half, slot, pl.ds(row, 16), m * 128 : m * 128 + 128] = values[m].astype(jnp.bfloat16)

                keep(t - 2 if t >= 2 else t + 7, rounded)
                keep(t + 2, shifted(rounded, 1))
                if t == 0:
                    keep(6, shifted(rounded, 2))
        return carry

    lax.fori_loop(0, 4, diffuse, 0)

    def respond(half, carry):
        for blk in range(2):
            for t in range(4):
                pieces = []
                for slot in range(t, t + 4):
                    if blk == 0:
                        pieces.append(dif[half, slot, 0:64, :])
                    else:
                        pieces.append(dif[half, slot, 16:32, :])
                        pieces.append(dif[half, slot, 48:96, :])
                part[0:192, :] = jnp.dot(
                    w2_ref[half, blk], jnp.concatenate(pieces, axis=0), preferred_element_type=jnp.float32
                )
                natural = t - 2 if t >= 2 else t + 7
                for g in range(2):
                    total = gathered(part, 32, g)
                    row = blk * 48 + g * 16
                    for m in range(8):
                        d = dif[half, natural, row : row + 16, m * 128 + 128 : m * 128 + 256].astype(jnp.float32)
                        final = d * (1.0 - total[m])
                        for o in range(2):
                            r0 = blk * 32 + g * 16 + o * 8
                            fin[t, pl.ds(r0 * 16 + (m % 2) * 8 + half * 4 + m // 2, 8, stride=16), :] = final[
                                o * 8 : o * 8 + 8
                            ]
        return carry

    lax.fori_loop(0, 2, respond, 0)

    def pack(d, c):
        base = pl.multiple_of(d * 32, 32)
        for t in range(4):
            a = fin[t, pl.ds(base, 32), :]
            swapped = jnp.concatenate([a[0:8], a[16:24], a[8:16], a[24:32]], axis=0)
            out_ref[d, :, t * 128 : t * 128 + 128] = swapped.astype(jnp.bfloat16)
        return c

    lax.fori_loop(0, 32, pack, 0)


def gathered(part, size, g):
    total = None
    for c1 in range(GROUPS):
        rows = c1 * size + g * 16
        tiles = shifted([part[rows : rows + 16, m * 128 : m * 128 + 128] for m in range(9)], c1 - 3)[1:]
        total = tiles if total is None else [a + b for a, b in zip(total, tiles)]
    return total


def exchange_photons(message_ref, out_ref, send_sem, recv_sem, own_sem, side_sem):
    sensor = lax.axis_index("sensor")
    band = lax.axis_index("rows")
    me = sensor * 4 + band
    barrier = pltpu.get_barrier_semaphore()

    def greet(k, c):
        peer = lax.rem(me + k, 128)
        pl.semaphore_signal(
            barrier, inc=1, device_id=(peer // 4, lax.rem(peer, 4)), device_id_type=pl.DeviceIdType.MESH
        )
        return c

    lax.fori_loop(1, 128, greet, 0)
    pl.semaphore_wait(barrier, 127)
    own = pltpu.make_async_copy(message_ref.at[me], out_ref.at[0, me], own_sem)
    own.start()

    def send(k, c):
        peer = lax.rem(me + k, 128)
        pltpu.make_async_remote_copy(
            src_ref=message_ref.at[peer],
            dst_ref=out_ref.at[0, me],
            send_sem=send_sem,
            recv_sem=recv_sem,
            device_id=(peer // 4, lax.rem(peer, 4)),
            device_id_type=pl.DeviceIdType.MESH,
        ).start()
        return c

    lax.fori_loop(1, 128, send, 0)
    own.wait()
    everything = pltpu.make_async_remote_copy(
        src_ref=message_ref.at[pl.ds(0, 127)],
        dst_ref=out_ref.at[0, pl.ds(0, 127)],
        send_sem=send_sem,
        recv_sem=recv_sem,
        device_id=(sensor, lax.rem(band + 1, 4)),
        device_id_type=pl.DeviceIdType.MESH,
    )
    everything.wait_recv()
    copies = []
    for side, to in ((1, 1), (2, 3)):
        copy = pltpu.make_async_remote_copy(
            src_ref=out_ref.at[0],
            dst_ref=out_ref.at[side],
            send_sem=side_sem.at[side - 1],
            recv_sem=side_sem.at[side + 1],
            device_id=(sensor, lax.rem(band + to, 4)),
            device_id_type=pl.DeviceIdType.MESH,
        )
        copy.start()
        copies.append(copy)
    everything.wait_send()
    for copy in copies:
        copy.wait()


def exchange_readout(block_ref, out_ref, send_sem, recv_sem, own_sem):
    me = lax.axis_index("sensor")
    band = lax.axis_index("rows")
    barrier = pltpu.get_barrier_semaphore()

    def greet(k, c):
        pl.semaphore_signal(
            barrier, inc=1, device_id=(lax.rem(me + k, 32), band), device_id_type=pl.DeviceIdType.MESH
        )
        return c

    lax.fori_loop(1, 32, greet, 0)
    pl.semaphore_wait(barrier, 31)
    own = pltpu.make_async_copy(block_ref.at[me], out_ref.at[me], own_sem)
    own.start()

    def send(k, c):
        peer = lax.rem(me + k, 32)
        pltpu.make_async_remote_copy(
            src_ref=block_ref.at[peer],
            dst_ref=out_ref.at[me],
            send_sem=send_sem,
            recv_sem=recv_sem,
            device_id=(peer, band),
            device_id_type=pl.DeviceIdType.MESH,
        ).start()
        return c

    lax.fori_loop(1, 32, send, 0)
    own.wait()
    everything = pltpu.make_async_remote_copy(
        src_ref=block_ref.at[pl.ds(0, 31)],
        dst_ref=out_ref.at[pl.ds(0, 31)],
        send_sem=send_sem,
        recv_sem=recv_sem,
        device_id=(lax.rem(me + 1, 32), band),
        device_id_type=pl.DeviceIdType.MESH,
    )
    everything.wait()


def crosstalk_kernel(got_ref, mix_ref, out_ref):
    source = lax.broadcasted_iota(jnp.int32, (512, 512), 0)
    column = lax.broadcasted_iota(jnp.int32, (512, 512), 1)
    place = (source & 127) * 4 + (source >> 7)
    even = (place == column).astype(jnp.bfloat16)
    odd = (511 - place == column).astype(jnp.bfloat16)
    for g in range(4):
        block = got_ref[g * 8 : g * 8 + 8]
        ordered = []
        for parity, order in ((0, even), (1, odd)):
            rows = block[:, parity * 16 : parity * 16 + 16, :].reshape(128, 512)
            ordered.append(jnp.dot(rows, order, preferred_element_type=jnp.float32).astype(jnp.bfloat16))
        mixed = jnp.dot(
            mix_ref[g], jnp.concatenate(ordered, axis=0), preferred_element_type=jnp.float32
        )
        for s in range(8):
            for r in range(2):
                for i0 in range(0, 16, 8):
                    for m in range(4):
                        row = s * 32 + r * 16 + i0
                        start = ((g * 8 + s) * 16 + i0) * 8 + m * 2 + r
                        out_ref[pl.ds(start, 8, stride=8), :] = mixed[row : row + 8, m * 128 : m * 128 + 128]


def shards(photon_charge, photon_pixel, photon_count, diffusion_kernel, fatter_kernel, crosstalk):
    vmem = pl.BlockSpec(memory_space=pltpu.VMEM)
    smem = pl.BlockSpec(memory_space=pltpu.SMEM)
    limit = pltpu.CompilerParams(vmem_limit_bytes=56 * 1024 * 1024)
    counts = photon_count[0]
    live = jnp.arange(32, dtype=jnp.int32)[None, :] < counts[:, None]
    charge = jnp.where(live[:, None, :], photon_charge[0], jnp.zeros((), jnp.bfloat16))
    message = jnp.concatenate(
        [charge.reshape(128, 96).astype(jnp.float32), photon_pixel[0].astype(jnp.float32)], axis=1
    )
    message = pl.pallas_call(
        order_slots,
        out_shape=jax.ShapeDtypeStruct((128, 128), jnp.float32),
        in_specs=[vmem],
        out_specs=vmem,
    )(message)
    lists = pl.pallas_call(
        exchange_photons,
        out_shape=jax.ShapeDtypeStruct((3, 128, 1, 128), jnp.float32),
        in_specs=[vmem],
        out_specs=vmem,
        scratch_shapes=[
            pltpu.SemaphoreType.DMA,
            pltpu.SemaphoreType.DMA,
            pltpu.SemaphoreType.DMA,
            pltpu.SemaphoreType.DMA((4,)),
        ],
        compiler_params=pltpu.CompilerParams(collective_id=0, has_side_effects=True),
    )(message.reshape(128, 1, 128)).reshape(3, 128, 128)
    band = lax.axis_index("rows")

    dk = jnp.pad(diffusion_kernel.astype(jnp.float32), ((0, 0), (0, 43), (0, 3)))
    dk = jnp.stack([dk, jnp.pad(jnp.flip(dk[:, :KSIZE], axis=1), ((0, 0), (0, 43), (0, 0)))])
    base1 = jnp.transpose(dk, (0, 3, 1, 2)).reshape(2, 36, 128)
    fk = jnp.pad(fatter_kernel.astype(jnp.float32), ((0, 43), (0, 3)))
    fk = jnp.stack([fk, jnp.pad(jnp.flip(fk[:KSIZE], axis=0), ((0, 43), (0, 0)))])
    base2 = jnp.transpose(fk, (0, 2, 1)).reshape(2, 12, 128)
    w1, w2, mix = pl.pallas_call(
        tables,
        out_shape=[
            jax.ShapeDtypeStruct((2, 2, 288, 768), jnp.bfloat16),
            jax.ShapeDtypeStruct((2, 2, 192, 256), jnp.bfloat16),
            jax.ShapeDtypeStruct((4, 256, 256), jnp.bfloat16),
        ],
        in_specs=[smem, vmem, vmem, vmem],
        out_specs=[vmem, vmem, vmem],
        cost_estimate=pl.CostEstimate(flops=10**8, bytes_accessed=4 * 10**6, transcendentals=0),
    )(band.reshape(1), base1, base2, crosstalk.reshape(512, 16))

    amplifiers = pl.pallas_call(
        photons_to_readout,
        out_shape=jax.ShapeDtypeStruct((32, 32, 512), jnp.bfloat16),
        in_specs=[smem, vmem, vmem, vmem],
        out_specs=vmem,
        scratch_shapes=[
            pltpu.VMEM((TRASH + 8, 128), jnp.float32),
            pltpu.VMEM((3, 256, 128), jnp.float32),
            pltpu.VMEM((3, 48, 128), jnp.int32),
            pltpu.SMEM((3, 48, 128), jnp.int32),
            pltpu.SMEM((LIST,), jnp.int32),
            pltpu.VMEM((7 * 192, WIDE), jnp.bfloat16),
            pltpu.VMEM((288, WIDE), jnp.float32),
            pltpu.VMEM((2, 9, 96, WIDE), jnp.bfloat16),
            pltpu.VMEM((4, 1024, 128), jnp.float32),
            pltpu.SemaphoreType.DMA,
        ],
        compiler_params=limit,
    )(band.reshape(1), lists, w1, w2)

    got = pl.pallas_call(
        exchange_readout,
        out_shape=jax.ShapeDtypeStruct((32, 32, 512), jnp.bfloat16),
        in_specs=[vmem],
        out_specs=vmem,
        scratch_shapes=[pltpu.SemaphoreType.DMA, pltpu.SemaphoreType.DMA, pltpu.SemaphoreType.DMA],
        compiler_params=pltpu.CompilerParams(collective_id=1, has_side_effects=True),
    )(amplifiers)
    flat = pl.pallas_call(
        crosstalk_kernel,
        out_shape=jax.ShapeDtypeStruct((4096, 128), jnp.float32),
        in_specs=[vmem, vmem],
        out_specs=vmem,
    )(got, mix)
    flat = flat.reshape(32, 16, 4, 2, 128)
    return jnp.transpose(flat, (0, 1, 3, 2, 4)).reshape(32, 16, 1, 2, 512)


def solution(mesh):
    placed = (
        P(("sensor", "rows"), None, None, None),
        P(("sensor", "rows"), None, None),
        P(("sensor", "rows"), None),
        P(),
        P(),
        P(),
    )
    return jax.shard_map(
        shards,
        mesh=mesh,
        in_specs=placed,
        out_specs=P(None, None, "rows", "sensor", None),
        check_vma=False,
    )
```

```python
import jax
import jax.numpy as jnp
from jax import lax
from jax.experimental import pallas as pl
from jax.experimental.pallas import tpu as pltpu
from jax.sharding import PartitionSpec as P

COLS = 4096
KSIZE = 21
READ_ROWS = 64
HALO = 20
EXT = READ_ROWS + 2 * HALO
TILE_ROWS = 2 * EXT * 4
TRASH = 32 * TILE_ROWS
GROUPS = 6
WIDE = 9 * 128
LIST = 4224
UNROLL = 16


def iota(shape, axis):
    return lax.broadcasted_iota(jnp.int32, shape, axis)


def order_slots(message_ref, out_ref):
    t = message_ref[...].T
    live = t[0:32] > 0.0
    r = (t[96:128].astype(jnp.int32) >> 12) & 63
    first = live & (r < HALO)
    final = live & (r >= READ_ROWS - HALO)
    inner = live & (r >= HALO) & (r < READ_ROWS - HALO)
    below = (iota((32, 32), 1) < iota((32, 32), 0)).astype(jnp.bfloat16)
    rank = jnp.zeros((32, 128), jnp.float32)
    offset = jnp.zeros((1, 128), jnp.float32)
    for member in (first, inner, final, jnp.logical_not(live)):
        ones = jnp.where(member, 1.0, 0.0)
        before = jnp.dot(below, ones.astype(jnp.bfloat16), preferred_element_type=jnp.float32)
        rank = jnp.where(member, before + offset, rank)
        offset = offset + jnp.sum(ones, axis=0, keepdims=True)
    rank = rank.astype(jnp.int32)
    place = iota((32, 128), 0)
    parts = [jnp.zeros((32, 128), jnp.float32)] * 4
    for s in range(32):
        here = place == rank[s : s + 1]
        parts = [p + jnp.where(here, t[c * 32 + s : c * 32 + s + 1], 0.0) for c, p in enumerate(parts)]
    out_ref[...] = jnp.concatenate(parts, axis=0).T


def tables(band_ref, base1_ref, base2_ref, cross_ref, w1_ref, w2_ref, mix_ref):
    band = band_ref[0]
    row8 = iota((8, 128), 0)
    for half in range(2):
        for c1 in range(GROUPS):
            for q in range(6):
                base = jnp.broadcast_to(base1_ref[half, c1 * 6 + q : c1 * 6 + q + 1, :], (8, 128))
                for blk in range(2):
                    rows = []
                    for g in range(6):
                        start = 2 + g * 8 if blk else (10 + g * 8 if g < 4 else (g - 4) * 8)
                        turned = pltpu.roll(base, start, axis=1, stride=1, stride_axis=0)
                        if g == 5:
                            turned = jnp.where(row8 < 2, turned, 0.0)
                        if blk == 0 and g >= 4:
                            turned = jnp.where(band == 0, 0.0, turned)
                        rows.append(turned)
                    w1_ref[half, blk, c1 * 48 : c1 * 48 + 48, q * 128 : q * 128 + 128] = jnp.concatenate(
                        rows, axis=0
                    ).astype(jnp.bfloat16)
            y = iota((8, 128), 1) & 63
            for q in range(2):
                base = jnp.broadcast_to(base2_ref[half, c1 * 2 + q : c1 * 2 + q + 1, :], (8, 128))
                first, second = [], []
                for g in range(4):

                    def turn(by, g=g, base=base):
                        return pltpu.roll(pltpu.roll(base, by, axis=1), g * 8, axis=1, stride=1, stride_axis=0)

                    late = turn(6)
                    second.append(late)
                    first.append(jnp.where(y < 32, turn(118), jnp.where(y < 48, turn(32), late)))
                for blk, rows in ((0, first), (1, second)):
                    w2_ref[half, blk, c1 * 32 : c1 * 32 + 32, q * 128 : q * 128 + 128] = jnp.concatenate(
                        rows, axis=0
                    ).astype(jnp.bfloat16)
    row = iota((256, 128), 0)
    source = iota((256, 128), 1)
    pick = (((row >> 5) * 16 + (row & 15)) == source).astype(jnp.bfloat16)
    column = iota((16, 256), 1)
    amp = ((column >> 2) & 1) * 8 + (column & 3) * 2 + (column >> 7)
    spread = (iota((16, 256), 0) == amp).astype(jnp.bfloat16)
    row = iota((256, 256), 0)
    column = iota((256, 256), 1)
    same = (row >> 4) == ((column >> 3) & 15)
    for g in range(4):
        wide = jnp.dot(
            cross_ref[g * 128 : g * 128 + 128, :], spread, preferred_element_type=jnp.float32
        ).astype(jnp.bfloat16)
        tall = jnp.dot(pick, wide, preferred_element_type=jnp.float32)
        mix_ref[g] = jnp.where(same, tall, 0.0).astype(jnp.bfloat16)


def shifted(tiles, by):
    if by == 0:
        return tiles
    lane = lax.broadcasted_iota(jnp.int32, tiles[0].shape, 1)
    zero = jnp.zeros_like(tiles[0])
    turned = [pltpu.roll(t, (-by) % 128, axis=1) for t in tiles]
    count = len(tiles)
    if by > 0:
        return [
            jnp.where(lane < 128 - by, turned[m], turned[m + 1] if m + 1 < count else zero)
            for m in range(count)
        ]
    return [jnp.where(lane < -by, turned[m - 1] if m else zero, turned[m]) for m in range(count)]


def photons_to_readout(
    band_ref, list_ref, w1_ref, w2_ref, out_ref,
    acc, dense, turned, key_v, key_s, flat0, flat1, flat2, bext, part, dif, fin, sem,
):
    band = band_ref[0]
    last = band == 3
    spread = iota((128, 128), 1)
    for q in range(3):
        t = list_ref[q]
        if q == 1:
            t = jnp.where(band == 0, 0.0, t)
        if q == 2:
            t = jnp.where(last, list_ref[0], t)
        live = (t > 0.0) & (spread < 32)
        pixel = pltpu.roll(t, 32, axis=1).astype(jnp.int32) & (2 * READ_ROWS * COLS - 1)
        u = pixel >> 12
        x = pixel & 4095
        half = u >> 6
        r = u & 63
        tile = (x & 3) * 8 + (x >> 9)
        lane = (x >> 2) & 127
        total = jnp.sum(jnp.where(live, 1, 0), axis=1, keepdims=True)
        heads = jnp.sum(jnp.where(live & (r < HALO), 1, 0), axis=1, keepdims=True)
        tails = jnp.sum(jnp.where(live & (r >= 44), 1, 0), axis=1, keepdims=True)
        if q == 0:
            row, first, many = r + HALO, jnp.zeros_like(total), total
        elif q == 1:
            row, first, many = r - 44, total - tails, tails
        else:
            row = jnp.where(last, 147 - r, 84 + r)
            half = jnp.where(last, 1 - half, half)
            first = jnp.where(last, total - tails, 0)
            many = jnp.where(last, tails, heads)
        e = half * EXT + row
        rot = (lane - iota((128, 128), 0)) & 127
        key = ((tile * EXT + (e >> 1)) << 20) + (((e & 1) * 128 + lane) << 12) + ((spread & 31) << 7) + rot
        for bit in range(5 if q else 0):
            key = jnp.where((first >> bit) & 1 == 1, pltpu.roll(key, 128 - (1 << bit), axis=1), key)
        key_v[q] = jnp.where(spread == 65, many, key)
    copy = pltpu.make_async_copy(key_v, key_s, sem)
    copy.start()
    for q in range(3):
        t = list_ref[q]
        if q == 1:
            t = jnp.where(band == 0, 0.0, t)
        if q == 2:
            t = jnp.where(last, list_ref[0], t)
        t = t.T
        dense[0:128, :] = t
        dense[128:256, :] = t
        for slot in range(32):
            turned[q, slot * 8 : slot * 8 + 8, :] = dense[pl.ds(slot, 8, stride=32), :]

    def clear(i, c):
        acc[pl.ds(pl.multiple_of(i * 512, 512), 512), :] = jnp.zeros((512, 128), jnp.float32)
        return c

    lax.fori_loop(0, TRASH // 512, clear, 0)
    acc[TRASH : TRASH + 8, :] = jnp.zeros((8, 128), jnp.float32)
    copy.wait()
    spot = (iota((8, 128), 1) + 128 * (iota((8, 128), 0) >> 2)) << 12
    flats = (flat0, flat1, flat2)
    steps = (16, 5, 5)

    def sender(i, at):
        many = [key_s[q, i, 65] for q in range(3)]
        read = [[key_s[q, i, v] for v in range(steps[q])] for q in range(3)]
        for q in range(3):
            for v, value in enumerate(read[q]):
                flats[q][at[q] + v] = value
        over = many[0] > steps[0]
        for q in (1, 2):
            over = over | (many[q] > steps[q])

        def rest(j, c):
            for q in range(3):
                values = [key_s[q, i, v] for v in range(steps[q], 32)]
                for v, value in enumerate(values):
                    flats[q][at[q] + steps[q] + v] = value
            return c

        lax.fori_loop(0, over.astype(jnp.int32), rest, 0)
        return tuple(a + m for a, m in zip(at, many))

    sizes = lax.fori_loop(0, 128, sender, (jnp.int32(0),) * 3)

    def finish(i, c):
        for q in range(3):
            flats[q][sizes[q] + i] = jnp.int32(((TRASH // 8) << 20) - (1 << 32))
        return c

    lax.fori_loop(0, 2 * UNROLL, finish, 0)
    for q in range(3):

        def prepare(j, q=q):
            bases, values = [], []
            for v in range(UNROLL):
                key = flats[q][j * UNROLL + v]
                bases.append(lax.shift_right_logical(key, 20))
                slot = pl.multiple_of((key >> 4) & 248, 8)
                moved = pltpu.roll(turned[q, pl.ds(slot, 8), :], key & 127, axis=1)
                target = jnp.full((8, 128), key, jnp.int32) & (255 << 12)
                values.append(jnp.where(spot == target, moved, 0.0))
            return tuple(bases), tuple(values)

        def add(j, carry, prepare=prepare):
            bases, values = carry
            following = prepare(j + 1)
            for v in range(0, UNROLL, 4):
                places = [pl.ds(pl.multiple_of(bases[v + w] * 8, 8), 8) for w in range(4)]
                sums = [acc[place, :] + values[v + w] for w, place in enumerate(places)]
                for w in range(1, 4):
                    for z in range(w):
                        same = bases[v + z] == bases[v + w]
                        sums[w] = sums[w] + jnp.where(same, values[v + z], 0.0)
                for place, value in zip(places, sums):
                    acc[place, :] = value
            return following

        lax.fori_loop(0, (sizes[q] + UNROLL - 1) // UNROLL, add, prepare(0))

    def diffuse(which, carry):
        half = which >> 1
        blk = which & 1
        start = (half * EXT + blk * 40) * 4
        pad = [jnp.zeros((64, 128), jnp.float32)]
        for p in range(4):
            for k in range(3):
                tiles = pad + [
                    acc[pl.ds((p * 8 + m) * TILE_ROWS + start + k, 64, stride=4), :] for m in range(8)
                ]

                def put(slot, values, k=k):
                    for m in range(9):
                        bext[slot * 192 + k * 64 : slot * 192 + k * 64 + 64, m * 128 : m * 128 + 128] = (
                            values[m].astype(jnp.bfloat16)
                        )

                if p >= 2:
                    put(p - 2, tiles)
                put(p + 2, shifted(tiles, 1))
                if p == 0:
                    put(6, shifted(tiles, 2))
        for t in range(4):
            part[...] = jnp.dot(
                w1_ref[half, blk], bext[t * 192 : (t + 4) * 192, :], preferred_element_type=jnp.float32
            )
            for g in range(3):
                total = gathered(part, 48, g)
                rounded = [jnp.zeros((16, 128), jnp.float32)] + [
                    v.astype(jnp.bfloat16).astype(jnp.float32) for v in total
                ]
                row = pl.multiple_of(blk * 48 + g * 16, 16)

                def keep(slot, values, row=row):
                    for m in range(9):
                        dif[half, slot, pl.ds(row, 16), m * 128 : m * 128 + 128] = values[m].astype(jnp.bfloat16)

                keep(t - 2 if t >= 2 else t + 7, rounded)
                keep(t + 2, shifted(rounded, 1))
                if t == 0:
                    keep(6, shifted(rounded, 2))
        return carry

    lax.fori_loop(0, 4, diffuse, 0)

    def respond(half, carry):
        for blk in range(2):
            for t in range(4):
                pieces = []
                for slot in range(t, t + 4):
                    if blk == 0:
                        pieces.append(dif[half, slot, 0:64, :])
                    else:
                        pieces.append(dif[half, slot, 16:32, :])
                        pieces.append(dif[half, slot, 48:96, :])
                part[0:192, :] = jnp.dot(
                    w2_ref[half, blk], jnp.concatenate(pieces, axis=0), preferred_element_type=jnp.float32
                )
                natural = t - 2 if t >= 2 else t + 7
                for g in range(2):
                    total = gathered(part, 32, g)
                    row = blk * 48 + g * 16
                    for m in range(8):
                        d = dif[half, natural, row : row + 16, m * 128 + 128 : m * 128 + 256].astype(jnp.float32)
                        final = d * (1.0 - total[m])
                        for o in range(2):
                            r0 = blk * 32 + g * 16 + o * 8
                            fin[t, pl.ds(r0 * 16 + (m % 2) * 8 + half * 4 + m // 2, 8, stride=16), :] = final[
                                o * 8 : o * 8 + 8
                            ]
        return carry

    lax.fori_loop(0, 2, respond, 0)

    def pack(d, c):
        base = pl.multiple_of(d * 32, 32)
        for t in range(4):
            a = fin[t, pl.ds(base, 32), :]
            swapped = jnp.concatenate([a[0:8], a[16:24], a[8:16], a[24:32]], axis=0)
            out_ref[d, :, t * 128 : t * 128 + 128] = swapped.astype(jnp.bfloat16)
        return c

    lax.fori_loop(0, 32, pack, 0)


def gathered(part, size, g):
    total = None
    for c1 in range(GROUPS):
        rows = c1 * size + g * 16
        tiles = shifted([part[rows : rows + 16, m * 128 : m * 128 + 128] for m in range(9)], c1 - 3)[1:]
        total = tiles if total is None else [a + b for a, b in zip(total, tiles)]
    return total


def exchange_photons(message_ref, out_ref, send_sem, recv_sem, own_sem, side_sem):
    sensor = lax.axis_index("sensor")
    band = lax.axis_index("rows")
    me = sensor * 4 + band
    barrier = pltpu.get_barrier_semaphore()

    def greet(k, c):
        peer = lax.rem(me + k, 128)
        pl.semaphore_signal(
            barrier, inc=1, device_id=(peer // 4, lax.rem(peer, 4)), device_id_type=pl.DeviceIdType.MESH
        )
        return c

    lax.fori_loop(1, 128, greet, 0)
    pl.semaphore_wait(barrier, 127)
    own = pltpu.make_async_copy(message_ref.at[me], out_ref.at[0, me], own_sem)
    own.start()

    def send(k, c):
        peer = lax.rem(me + k, 128)
        pltpu.make_async_remote_copy(
            src_ref=message_ref.at[peer],
            dst_ref=out_ref.at[0, me],
            send_sem=send_sem,
            recv_sem=recv_sem,
            device_id=(peer // 4, lax.rem(peer, 4)),
            device_id_type=pl.DeviceIdType.MESH,
        ).start()
        return c

    lax.fori_loop(1, 128, send, 0)
    own.wait()
    everything = pltpu.make_async_remote_copy(
        src_ref=message_ref.at[pl.ds(0, 127)],
        dst_ref=out_ref.at[0, pl.ds(0, 127)],
        send_sem=send_sem,
        recv_sem=recv_sem,
        device_id=(sensor, lax.rem(band + 1, 4)),
        device_id_type=pl.DeviceIdType.MESH,
    )
    everything.wait_recv()
    copies = []
    for side, to in ((1, 1), (2, 3)):
        copy = pltpu.make_async_remote_copy(
            src_ref=out_ref.at[0],
            dst_ref=out_ref.at[side],
            send_sem=side_sem.at[side - 1],
            recv_sem=side_sem.at[side + 1],
            device_id=(sensor, lax.rem(band + to, 4)),
            device_id_type=pl.DeviceIdType.MESH,
        )
        copy.start()
        copies.append(copy)
    everything.wait_send()
    for copy in copies:
        copy.wait()


def exchange_readout(block_ref, out_ref, send_sem, recv_sem, own_sem):
    me = lax.axis_index("sensor")
    band = lax.axis_index("rows")
    barrier = pltpu.get_barrier_semaphore()

    def greet(k, c):
        pl.semaphore_signal(
            barrier, inc=1, device_id=(lax.rem(me + k, 32), band), device_id_type=pl.DeviceIdType.MESH
        )
        return c

    lax.fori_loop(1, 32, greet, 0)
    pl.semaphore_wait(barrier, 31)
    own = pltpu.make_async_copy(block_ref.at[me], out_ref.at[me], own_sem)
    own.start()

    def send(k, c):
        peer = lax.rem(me + k, 32)
        pltpu.make_async_remote_copy(
            src_ref=block_ref.at[peer],
            dst_ref=out_ref.at[me],
            send_sem=send_sem,
            recv_sem=recv_sem,
            device_id=(peer, band),
            device_id_type=pl.DeviceIdType.MESH,
        ).start()
        return c

    lax.fori_loop(1, 32, send, 0)
    own.wait()
    everything = pltpu.make_async_remote_copy(
        src_ref=block_ref.at[pl.ds(0, 31)],
        dst_ref=out_ref.at[pl.ds(0, 31)],
        send_sem=send_sem,
        recv_sem=recv_sem,
        device_id=(lax.rem(me + 1, 32), band),
        device_id_type=pl.DeviceIdType.MESH,
    )
    everything.wait()


def crosstalk_kernel(got_ref, mix_ref, out_ref):
    source = lax.broadcasted_iota(jnp.int32, (512, 512), 0)
    column = lax.broadcasted_iota(jnp.int32, (512, 512), 1)
    place = (source & 127) * 4 + (source >> 7)
    even = (place == column).astype(jnp.bfloat16)
    odd = (511 - place == column).astype(jnp.bfloat16)
    for g in range(4):
        block = got_ref[g * 8 : g * 8 + 8]
        ordered = []
        for parity, order in ((0, even), (1, odd)):
            rows = block[:, parity * 16 : parity * 16 + 16, :].reshape(128, 512)
            ordered.append(jnp.dot(rows, order, preferred_element_type=jnp.float32).astype(jnp.bfloat16))
        mixed = jnp.dot(
            mix_ref[g], jnp.concatenate(ordered, axis=0), preferred_element_type=jnp.float32
        )
        for s in range(8):
            for r in range(2):
                for i0 in range(0, 16, 8):
                    for m in range(4):
                        row = s * 32 + r * 16 + i0
                        start = ((g * 8 + s) * 16 + i0) * 8 + m * 2 + r
                        out_ref[pl.ds(start, 8, stride=8), :] = mixed[row : row + 8, m * 128 : m * 128 + 128]


def shards(photon_charge, photon_pixel, photon_count, diffusion_kernel, fatter_kernel, crosstalk):
    vmem = pl.BlockSpec(memory_space=pltpu.VMEM)
    smem = pl.BlockSpec(memory_space=pltpu.SMEM)
    limit = pltpu.CompilerParams(vmem_limit_bytes=56 * 1024 * 1024)
    counts = photon_count[0]
    live = jnp.arange(32, dtype=jnp.int32)[None, :] < counts[:, None]
    charge = jnp.where(live[:, None, :], photon_charge[0], jnp.zeros((), jnp.bfloat16))
    message = jnp.concatenate(
        [charge.reshape(128, 96).astype(jnp.float32), photon_pixel[0].astype(jnp.float32)], axis=1
    )
    message = pl.pallas_call(
        order_slots,
        out_shape=jax.ShapeDtypeStruct((128, 128), jnp.float32),
        in_specs=[vmem],
        out_specs=vmem,
    )(message)
    lists = pl.pallas_call(
        exchange_photons,
        out_shape=jax.ShapeDtypeStruct((3, 128, 1, 128), jnp.float32),
        in_specs=[vmem],
        out_specs=vmem,
        scratch_shapes=[
            pltpu.SemaphoreType.DMA,
            pltpu.SemaphoreType.DMA,
            pltpu.SemaphoreType.DMA,
            pltpu.SemaphoreType.DMA((4,)),
        ],
        compiler_params=pltpu.CompilerParams(collective_id=0, has_side_effects=True),
    )(message.reshape(128, 1, 128)).reshape(3, 128, 128)
    band = lax.axis_index("rows")

    dk = jnp.pad(diffusion_kernel.astype(jnp.float32), ((0, 0), (0, 43), (0, 3)))
    dk = jnp.stack([dk, jnp.pad(jnp.flip(dk[:, :KSIZE], axis=1), ((0, 0), (0, 43), (0, 0)))])
    base1 = jnp.transpose(dk, (0, 3, 1, 2)).reshape(2, 36, 128)
    fk = jnp.pad(fatter_kernel.astype(jnp.float32), ((0, 43), (0, 3)))
    fk = jnp.stack([fk, jnp.pad(jnp.flip(fk[:KSIZE], axis=0), ((0, 43), (0, 0)))])
    base2 = jnp.transpose(fk, (0, 2, 1)).reshape(2, 12, 128)
    w1, w2, mix = pl.pallas_call(
        tables,
        out_shape=[
            jax.ShapeDtypeStruct((2, 2, 288, 768), jnp.bfloat16),
            jax.ShapeDtypeStruct((2, 2, 192, 256), jnp.bfloat16),
            jax.ShapeDtypeStruct((4, 256, 256), jnp.bfloat16),
        ],
        in_specs=[smem, vmem, vmem, vmem],
        out_specs=[vmem, vmem, vmem],
        cost_estimate=pl.CostEstimate(flops=10**8, bytes_accessed=4 * 10**6, transcendentals=0),
    )(band.reshape(1), base1, base2, crosstalk.reshape(512, 16))

    amplifiers = pl.pallas_call(
        photons_to_readout,
        out_shape=jax.ShapeDtypeStruct((32, 32, 512), jnp.bfloat16),
        in_specs=[smem, vmem, vmem, vmem],
        out_specs=vmem,
        scratch_shapes=[
            pltpu.VMEM((TRASH + 8, 128), jnp.float32),
            pltpu.VMEM((256, 128), jnp.float32),
            pltpu.VMEM((3, 256, 128), jnp.float32),
            pltpu.VMEM((3, 128, 128), jnp.int32),
            pltpu.SMEM((3, 128, 128), jnp.int32),
            pltpu.SMEM((LIST,), jnp.int32),
            pltpu.SMEM((LIST,), jnp.int32),
            pltpu.SMEM((LIST,), jnp.int32),
            pltpu.VMEM((7 * 192, WIDE), jnp.bfloat16),
            pltpu.VMEM((288, WIDE), jnp.float32),
            pltpu.VMEM((2, 9, 96, WIDE), jnp.bfloat16),
            pltpu.VMEM((4, 1024, 128), jnp.float32),
            pltpu.SemaphoreType.DMA,
        ],
        compiler_params=limit,
    )(band.reshape(1), lists, w1, w2)

    got = pl.pallas_call(
        exchange_readout,
        out_shape=jax.ShapeDtypeStruct((32, 32, 512), jnp.bfloat16),
        in_specs=[vmem],
        out_specs=vmem,
        scratch_shapes=[pltpu.SemaphoreType.DMA, pltpu.SemaphoreType.DMA, pltpu.SemaphoreType.DMA],
        compiler_params=pltpu.CompilerParams(collective_id=1, has_side_effects=True),
    )(amplifiers)
    flat = pl.pallas_call(
        crosstalk_kernel,
        out_shape=jax.ShapeDtypeStruct((4096, 128), jnp.float32),
        in_specs=[vmem, vmem],
        out_specs=vmem,
    )(got, mix)
    flat = flat.reshape(32, 16, 4, 2, 128)
    return jnp.transpose(flat, (0, 1, 3, 2, 4)).reshape(32, 16, 1, 2, 512)


def solution(mesh):
    placed = (
        P(("sensor", "rows"), None, None, None),
        P(("sensor", "rows"), None, None),
        P(("sensor", "rows"), None),
        P(),
        P(),
        P(),
    )
    return jax.shard_map(
        shards,
        mesh=mesh,
        in_specs=placed,
        out_specs=P(None, None, "rows", "sensor", None),
        check_vma=False,
    )
```

```python
import jax
import jax.numpy as jnp
from jax import lax
from jax.experimental import pallas as pl
from jax.experimental.pallas import tpu as pltpu
from jax.sharding import PartitionSpec as P

COLS = 4096
KSIZE = 21
READ_ROWS = 64
HALO = 20
EXT = READ_ROWS + 2 * HALO
TILE_ROWS = 2 * EXT * 4
TRASH = 32 * TILE_ROWS
GROUPS = 6
WIDE = 9 * 128
LIST = 4224
UNROLL = 16


def iota(shape, axis):
    return lax.broadcasted_iota(jnp.int32, shape, axis)


def order_slots(message_ref, out_ref):
    t = message_ref[...].T
    live = t[0:32] > 0.0
    r = (t[96:128].astype(jnp.int32) >> 12) & 63
    first = live & (r < HALO)
    final = live & (r >= READ_ROWS - HALO)
    inner = live & (r >= HALO) & (r < READ_ROWS - HALO)
    below = (iota((32, 32), 1) < iota((32, 32), 0)).astype(jnp.bfloat16)
    rank = jnp.zeros((32, 128), jnp.float32)
    offset = jnp.zeros((1, 128), jnp.float32)
    for member in (first, inner, final, jnp.logical_not(live)):
        ones = jnp.where(member, 1.0, 0.0)
        before = jnp.dot(below, ones.astype(jnp.bfloat16), preferred_element_type=jnp.float32)
        rank = jnp.where(member, before + offset, rank)
        offset = offset + jnp.sum(ones, axis=0, keepdims=True)
    rank = rank.astype(jnp.int32)
    place = iota((32, 128), 0)
    parts = [jnp.zeros((32, 128), jnp.float32)] * 4
    for s in range(32):
        here = place == rank[s : s + 1]
        parts = [p + jnp.where(here, t[c * 32 + s : c * 32 + s + 1], 0.0) for c, p in enumerate(parts)]
    out_ref[...] = jnp.concatenate(parts, axis=0).T


def tables(band_ref, base1_ref, base2_ref, cross_ref, w1_ref, w2_ref, mix_ref):
    band = band_ref[0]
    row8 = iota((8, 128), 0)
    for half in range(2):
        for c1 in range(GROUPS):
            for q in range(6):
                base = jnp.broadcast_to(base1_ref[half, c1 * 6 + q : c1 * 6 + q + 1, :], (8, 128))
                for blk in range(2):
                    rows = []
                    for g in range(6):
                        start = 2 + g * 8 if blk else (10 + g * 8 if g < 4 else (g - 4) * 8)
                        turned = pltpu.roll(base, start, axis=1, stride=1, stride_axis=0)
                        if g == 5:
                            turned = jnp.where(row8 < 2, turned, 0.0)
                        if blk == 0 and g >= 4:
                            turned = jnp.where(band == 0, 0.0, turned)
                        rows.append(turned)
                    w1_ref[half, blk, c1 * 48 : c1 * 48 + 48, q * 128 : q * 128 + 128] = jnp.concatenate(
                        rows, axis=0
                    ).astype(jnp.bfloat16)
            y = iota((8, 128), 1) & 63
            for q in range(2):
                base = jnp.broadcast_to(base2_ref[half, c1 * 2 + q : c1 * 2 + q + 1, :], (8, 128))
                first, second = [], []
                for g in range(4):

                    def turn(by, g=g, base=base):
                        return pltpu.roll(pltpu.roll(base, by, axis=1), g * 8, axis=1, stride=1, stride_axis=0)

                    late = turn(6)
                    second.append(late)
                    first.append(jnp.where(y < 32, turn(118), jnp.where(y < 48, turn(32), late)))
                for blk, rows in ((0, first), (1, second)):
                    w2_ref[half, blk, c1 * 32 : c1 * 32 + 32, q * 128 : q * 128 + 128] = jnp.concatenate(
                        rows, axis=0
                    ).astype(jnp.bfloat16)
    row = iota((256, 128), 0)
    source = iota((256, 128), 1)
    pick = (((row >> 5) * 16 + (row & 15)) == source).astype(jnp.bfloat16)
    column = iota((16, 256), 1)
    amp = ((column >> 2) & 1) * 8 + (column & 3) * 2 + (column >> 7)
    spread = (iota((16, 256), 0) == amp).astype(jnp.bfloat16)
    row = iota((256, 256), 0)
    column = iota((256, 256), 1)
    same = (row >> 4) == ((column >> 3) & 15)
    for g in range(4):
        wide = jnp.dot(
            cross_ref[g * 128 : g * 128 + 128, :], spread, preferred_element_type=jnp.float32
        ).astype(jnp.bfloat16)
        tall = jnp.dot(pick, wide, preferred_element_type=jnp.float32)
        mix_ref[g] = jnp.where(same, tall, 0.0).astype(jnp.bfloat16)


def shifted(tiles, by):
    if by == 0:
        return tiles
    lane = lax.broadcasted_iota(jnp.int32, tiles[0].shape, 1)
    zero = jnp.zeros_like(tiles[0])
    turned = [pltpu.roll(t, (-by) % 128, axis=1) for t in tiles]
    count = len(tiles)
    if by > 0:
        return [
            jnp.where(lane < 128 - by, turned[m], turned[m + 1] if m + 1 < count else zero)
            for m in range(count)
        ]
    return [jnp.where(lane < -by, turned[m - 1] if m else zero, turned[m]) for m in range(count)]


def photons_to_readout(
    band_ref, list_ref, w1_ref, w2_ref, out_ref,
    acc, dense, turned, key_v, key_s, flat0, flat1, flat2, bext, part, dif, fin, sem,
):
    band = band_ref[0]
    last = band == 3
    spread = iota((128, 128), 1)
    for q in range(3):
        t = list_ref[q]
        if q == 1:
            t = jnp.where(band == 0, 0.0, t)
        if q == 2:
            t = jnp.where(last, list_ref[0], t)
        live = (t > 0.0) & (spread < 32)
        pixel = pltpu.roll(t, 32, axis=1).astype(jnp.int32) & (2 * READ_ROWS * COLS - 1)
        u = pixel >> 12
        x = pixel & 4095
        half = u >> 6
        r = u & 63
        tile = (x & 3) * 8 + (x >> 9)
        lane = (x >> 2) & 127
        total = jnp.sum(jnp.where(live, 1, 0), axis=1, keepdims=True)
        heads = jnp.sum(jnp.where(live & (r < HALO), 1, 0), axis=1, keepdims=True)
        tails = jnp.sum(jnp.where(live & (r >= 44), 1, 0), axis=1, keepdims=True)
        if q == 0:
            row, first, many = r + HALO, jnp.zeros_like(total), total
        elif q == 1:
            row, first, many = r - 44, total - tails, tails
        else:
            row = jnp.where(last, 147 - r, 84 + r)
            half = jnp.where(last, 1 - half, half)
            first = jnp.where(last, total - tails, 0)
            many = jnp.where(last, tails, heads)
        e = half * EXT + row
        rot = (lane - iota((128, 128), 0)) & 127
        key = ((tile * EXT + (e >> 1)) << 20) + (((e & 1) * 128 + lane) << 12) + ((spread & 31) << 7) + rot
        for bit in range(5 if q else 0):
            key = jnp.where((first >> bit) & 1 == 1, pltpu.roll(key, 128 - (1 << bit), axis=1), key)
        key_v[q] = jnp.where(spread == 65, many, key)
    copy = pltpu.make_async_copy(key_v, key_s, sem)
    copy.start()
    for q in range(3):
        t = list_ref[q]
        if q == 1:
            t = jnp.where(band == 0, 0.0, t)
        if q == 2:
            t = jnp.where(last, list_ref[0], t)
        t = t.T
        dense[0:128, :] = t
        dense[128:256, :] = t
        for slot in range(32):
            turned[q, slot * 8 : slot * 8 + 8, :] = dense[pl.ds(slot, 8, stride=32), :]

    def clear(i, c):
        acc[pl.ds(pl.multiple_of(i * 512, 512), 512), :] = jnp.zeros((512, 128), jnp.float32)
        return c

    lax.fori_loop(0, TRASH // 512, clear, 0)
    acc[TRASH : TRASH + 8, :] = jnp.zeros((8, 128), jnp.float32)
    copy.wait()
    spot = (iota((8, 128), 1) + 128 * (iota((8, 128), 0) >> 2)) << 12
    flats = (flat0, flat1, flat2)
    steps = (16, 5, 5)

    def sender(i, at):
        many = [key_s[q, i, 65] for q in range(3)]
        read = [[key_s[q, i, v] for v in range(steps[q])] for q in range(3)]
        for q in range(3):
            for v, value in enumerate(read[q]):
                flats[q][at[q] + v] = value
        for q in range(3):

            def rest(j, c, q=q):
                values = [key_s[q, i, v] for v in range(steps[q], 32)]
                for v, value in enumerate(values):
                    flats[q][at[q] + steps[q] + v] = value
                return c

            lax.fori_loop(0, (many[q] > steps[q]).astype(jnp.int32), rest, 0)

        return tuple(a + m for a, m in zip(at, many))

    sizes = lax.fori_loop(0, 128, sender, (jnp.int32(0),) * 3)

    def finish(i, c):
        for q in range(3):
            flats[q][sizes[q] + i] = jnp.int32(((TRASH // 8) << 20) - (1 << 32))
        return c

    lax.fori_loop(0, 2 * UNROLL, finish, 0)
    for q in range(3):

        def prepare(j, q=q):
            bases, values = [], []
            for v in range(UNROLL):
                key = flats[q][j * UNROLL + v]
                bases.append(lax.shift_right_logical(key, 20))
                slot = pl.multiple_of((key >> 4) & 248, 8)
                moved = pltpu.roll(turned[q, pl.ds(slot, 8), :], key & 127, axis=1)
                target = jnp.full((8, 128), key, jnp.int32) & (255 << 12)
                values.append(jnp.where(spot == target, moved, 0.0))
            return tuple(bases), tuple(values)

        def add(j, carry, prepare=prepare):
            bases, values = carry
            following = prepare(j + 1)
            for v in range(0, UNROLL, 4):
                places = [pl.ds(pl.multiple_of(bases[v + w] * 8, 8), 8) for w in range(4)]
                sums = [acc[place, :] + values[v + w] for w, place in enumerate(places)]
                for w in range(1, 4):
                    for z in range(w):
                        same = bases[v + z] == bases[v + w]
                        sums[w] = sums[w] + jnp.where(same, values[v + z], 0.0)
                for place, value in zip(places, sums):
                    acc[place, :] = value
            return following

        lax.fori_loop(0, (sizes[q] + UNROLL - 1) // UNROLL, add, prepare(0))

    def diffuse(which, carry):
        half = which >> 1
        blk = which & 1
        start = (half * EXT + blk * 40) * 4
        pad = [jnp.zeros((64, 128), jnp.float32)]
        for p in range(4):
            for k in range(3):
                tiles = pad + [
                    acc[pl.ds((p * 8 + m) * TILE_ROWS + start + k, 64, stride=4), :] for m in range(8)
                ]

                def put(slot, values, k=k):
                    for m in range(9):
                        bext[slot * 192 + k * 64 : slot * 192 + k * 64 + 64, m * 128 : m * 128 + 128] = (
                            values[m].astype(jnp.bfloat16)
                        )

                if p >= 2:
                    put(p - 2, tiles)
                put(p + 2, shifted(tiles, 1))
                if p == 0:
                    put(6, shifted(tiles, 2))
        for t in range(4):
            part[...] = jnp.dot(
                w1_ref[half, blk], bext[t * 192 : (t + 4) * 192, :], preferred_element_type=jnp.float32
            )
            for g in range(3):
                total = gathered(part, 48, g)
                rounded = [jnp.zeros((16, 128), jnp.float32)] + [
                    v.astype(jnp.bfloat16).astype(jnp.float32) for v in total
                ]
                row = pl.multiple_of(blk * 48 + g * 16, 16)

                def keep(slot, values, row=row):
                    for m in range(9):
                        dif[half, slot, pl.ds(row, 16), m * 128 : m * 128 + 128] = values[m].astype(jnp.bfloat16)

                keep(t - 2 if t >= 2 else t + 7, rounded)
                keep(t + 2, shifted(rounded, 1))
                if t == 0:
                    keep(6, shifted(rounded, 2))
        return carry

    lax.fori_loop(0, 4, diffuse, 0)

    def respond(half, carry):
        for blk in range(2):
            for t in range(4):
                pieces = []
                for slot in range(t, t + 4):
                    if blk == 0:
                        pieces.append(dif[half, slot, 0:64, :])
                    else:
                        pieces.append(dif[half, slot, 16:32, :])
                        pieces.append(dif[half, slot, 48:96, :])
                part[0:192, :] = jnp.dot(
                    w2_ref[half, blk], jnp.concatenate(pieces, axis=0), preferred_element_type=jnp.float32
                )
                natural = t - 2 if t >= 2 else t + 7
                for g in range(2):
                    total = gathered(part, 32, g)
                    row = blk * 48 + g * 16
                    for m in range(8):
                        d = dif[half, natural, row : row + 16, m * 128 + 128 : m * 128 + 256].astype(jnp.float32)
                        final = d * (1.0 - total[m])
                        for o in range(2):
                            r0 = blk * 32 + g * 16 + o * 8
                            fin[t, pl.ds(r0 * 16 + (m % 2) * 8 + half * 4 + m // 2, 8, stride=16), :] = final[
                                o * 8 : o * 8 + 8
                            ]
        return carry

    lax.fori_loop(0, 2, respond, 0)

    def pack(d, c):
        base = pl.multiple_of(d * 32, 32)
        for t in range(4):
            a = fin[t, pl.ds(base, 32), :]
            swapped = jnp.concatenate([a[0:8], a[16:24], a[8:16], a[24:32]], axis=0)
            out_ref[d, :, t * 128 : t * 128 + 128] = swapped.astype(jnp.bfloat16)
        return c

    lax.fori_loop(0, 32, pack, 0)


def gathered(part, size, g):
    total = None
    for c1 in range(GROUPS):
        rows = c1 * size + g * 16
        tiles = shifted([part[rows : rows + 16, m * 128 : m * 128 + 128] for m in range(9)], c1 - 3)[1:]
        total = tiles if total is None else [a + b for a, b in zip(total, tiles)]
    return total


def exchange_photons(message_ref, out_ref, send_sem, recv_sem, own_sem, side_sem):
    sensor = lax.axis_index("sensor")
    band = lax.axis_index("rows")
    me = sensor * 4 + band
    barrier = pltpu.get_barrier_semaphore()

    bands = [lax.rem(band + step, 4) for step in range(4)]

    def each(act):
        for to in bands[1:]:
            act(sensor, to)

        def others(k, c):
            target = lax.rem(sensor + k * 11, 32)
            for to in bands:
                act(target, to)
            return c

        lax.fori_loop(1, 32, others, 0)

    def greet(target, to):
        pl.semaphore_signal(barrier, inc=1, device_id=(target, to), device_id_type=pl.DeviceIdType.MESH)

    def send(target, to):
        pltpu.make_async_remote_copy(
            src_ref=message_ref.at[target * 4 + to],
            dst_ref=out_ref.at[0, me],
            send_sem=send_sem,
            recv_sem=recv_sem,
            device_id=(target, to),
            device_id_type=pl.DeviceIdType.MESH,
        ).start()

    each(greet)
    own = pltpu.make_async_copy(message_ref.at[me], out_ref.at[0, me], own_sem)
    own.start()
    pl.semaphore_wait(barrier, 127)
    each(send)
    own.wait()
    everything = pltpu.make_async_remote_copy(
        src_ref=message_ref.at[pl.ds(0, 127)],
        dst_ref=out_ref.at[0, pl.ds(0, 127)],
        send_sem=send_sem,
        recv_sem=recv_sem,
        device_id=(sensor, lax.rem(band + 1, 4)),
        device_id_type=pl.DeviceIdType.MESH,
    )
    everything.wait_recv()
    copies = []
    for side, to in ((1, 1), (2, 3)):
        copy = pltpu.make_async_remote_copy(
            src_ref=out_ref.at[0],
            dst_ref=out_ref.at[side],
            send_sem=side_sem.at[side - 1],
            recv_sem=side_sem.at[side + 1],
            device_id=(sensor, lax.rem(band + to, 4)),
            device_id_type=pl.DeviceIdType.MESH,
        )
        copy.start()
        copies.append(copy)
    everything.wait_send()
    for copy in copies:
        copy.wait()


def exchange_readout(block_ref, out_ref, send_sem, recv_sem, own_sem):
    me = lax.axis_index("sensor")
    band = lax.axis_index("rows")
    barrier = pltpu.get_barrier_semaphore()

    def greet(k, c):
        pl.semaphore_signal(
            barrier, inc=1, device_id=(lax.rem(me + k, 32), band), device_id_type=pl.DeviceIdType.MESH
        )
        return c

    lax.fori_loop(1, 32, greet, 0)
    pl.semaphore_wait(barrier, 31)
    own = pltpu.make_async_copy(block_ref.at[me], out_ref.at[me], own_sem)
    own.start()

    def send(k, c):
        peer = lax.rem(me + k * 11, 32)
        pltpu.make_async_remote_copy(
            src_ref=block_ref.at[peer],
            dst_ref=out_ref.at[me],
            send_sem=send_sem,
            recv_sem=recv_sem,
            device_id=(peer, band),
            device_id_type=pl.DeviceIdType.MESH,
        ).start()
        return c

    lax.fori_loop(1, 32, send, 0)
    own.wait()
    everything = pltpu.make_async_remote_copy(
        src_ref=block_ref.at[pl.ds(0, 31)],
        dst_ref=out_ref.at[pl.ds(0, 31)],
        send_sem=send_sem,
        recv_sem=recv_sem,
        device_id=(lax.rem(me + 1, 32), band),
        device_id_type=pl.DeviceIdType.MESH,
    )
    everything.wait()


def crosstalk_kernel(got_ref, mix_ref, out_ref):
    source = lax.broadcasted_iota(jnp.int32, (512, 512), 0)
    column = lax.broadcasted_iota(jnp.int32, (512, 512), 1)
    place = (source & 127) * 4 + (source >> 7)
    even = (place == column).astype(jnp.bfloat16)
    odd = (511 - place == column).astype(jnp.bfloat16)
    for g in range(4):
        block = got_ref[g * 8 : g * 8 + 8]
        ordered = []
        for parity, order in ((0, even), (1, odd)):
            rows = block[:, parity * 16 : parity * 16 + 16, :].reshape(128, 512)
            ordered.append(jnp.dot(rows, order, preferred_element_type=jnp.float32).astype(jnp.bfloat16))
        mixed = jnp.dot(
            mix_ref[g], jnp.concatenate(ordered, axis=0), preferred_element_type=jnp.float32
        )
        for s in range(8):
            for r in range(2):
                for i0 in range(0, 16, 8):
                    for m in range(4):
                        row = s * 32 + r * 16 + i0
                        start = ((g * 8 + s) * 16 + i0) * 8 + m * 2 + r
                        out_ref[pl.ds(start, 8, stride=8), :] = mixed[row : row + 8, m * 128 : m * 128 + 128]


def shards(photon_charge, photon_pixel, photon_count, diffusion_kernel, fatter_kernel, crosstalk):
    vmem = pl.BlockSpec(memory_space=pltpu.VMEM)
    smem = pl.BlockSpec(memory_space=pltpu.SMEM)
    limit = pltpu.CompilerParams(vmem_limit_bytes=56 * 1024 * 1024)
    counts = photon_count[0]
    live = jnp.arange(32, dtype=jnp.int32)[None, :] < counts[:, None]
    charge = jnp.where(live[:, None, :], photon_charge[0], jnp.zeros((), jnp.bfloat16))
    message = jnp.concatenate(
        [charge.reshape(128, 96).astype(jnp.float32), photon_pixel[0].astype(jnp.float32)], axis=1
    )
    message = pl.pallas_call(
        order_slots,
        out_shape=jax.ShapeDtypeStruct((128, 128), jnp.float32),
        in_specs=[vmem],
        out_specs=vmem,
    )(message)
    lists = pl.pallas_call(
        exchange_photons,
        out_shape=jax.ShapeDtypeStruct((3, 128, 1, 128), jnp.float32),
        in_specs=[vmem],
        out_specs=vmem,
        scratch_shapes=[
            pltpu.SemaphoreType.DMA,
            pltpu.SemaphoreType.DMA,
            pltpu.SemaphoreType.DMA,
            pltpu.SemaphoreType.DMA((4,)),
        ],
        compiler_params=pltpu.CompilerParams(collective_id=0, has_side_effects=True),
    )(message.reshape(128, 1, 128)).reshape(3, 128, 128)
    band = lax.axis_index("rows")

    dk = jnp.pad(diffusion_kernel.astype(jnp.float32), ((0, 0), (0, 43), (0, 3)))
    dk = jnp.stack([dk, jnp.pad(jnp.flip(dk[:, :KSIZE], axis=1), ((0, 0), (0, 43), (0, 0)))])
    base1 = jnp.transpose(dk, (0, 3, 1, 2)).reshape(2, 36, 128)
    fk = jnp.pad(fatter_kernel.astype(jnp.float32), ((0, 43), (0, 3)))
    fk = jnp.stack([fk, jnp.pad(jnp.flip(fk[:KSIZE], axis=0), ((0, 43), (0, 0)))])
    base2 = jnp.transpose(fk, (0, 2, 1)).reshape(2, 12, 128)
    w1, w2, mix = pl.pallas_call(
        tables,
        out_shape=[
            jax.ShapeDtypeStruct((2, 2, 288, 768), jnp.bfloat16),
            jax.ShapeDtypeStruct((2, 2, 192, 256), jnp.bfloat16),
            jax.ShapeDtypeStruct((4, 256, 256), jnp.bfloat16),
        ],
        in_specs=[smem, vmem, vmem, vmem],
        out_specs=[vmem, vmem, vmem],
        cost_estimate=pl.CostEstimate(flops=10**8, bytes_accessed=4 * 10**6, transcendentals=0),
    )(band.reshape(1), base1, base2, crosstalk.reshape(512, 16))

    amplifiers = pl.pallas_call(
        photons_to_readout,
        out_shape=jax.ShapeDtypeStruct((32, 32, 512), jnp.bfloat16),
        in_specs=[smem, vmem, vmem, vmem],
        out_specs=vmem,
        scratch_shapes=[
            pltpu.VMEM((TRASH + 8, 128), jnp.float32),
            pltpu.VMEM((256, 128), jnp.float32),
            pltpu.VMEM((3, 256, 128), jnp.float32),
            pltpu.VMEM((3, 128, 128), jnp.int32),
            pltpu.SMEM((3, 128, 128), jnp.int32),
            pltpu.SMEM((LIST,), jnp.int32),
            pltpu.SMEM((LIST,), jnp.int32),
            pltpu.SMEM((LIST,), jnp.int32),
            pltpu.VMEM((7 * 192, WIDE), jnp.bfloat16),
            pltpu.VMEM((288, WIDE), jnp.float32),
            pltpu.VMEM((2, 9, 96, WIDE), jnp.bfloat16),
            pltpu.VMEM((4, 1024, 128), jnp.float32),
            pltpu.SemaphoreType.DMA,
        ],
        compiler_params=limit,
    )(band.reshape(1), lists, w1, w2)

    got = pl.pallas_call(
        exchange_readout,
        out_shape=jax.ShapeDtypeStruct((32, 32, 512), jnp.bfloat16),
        in_specs=[vmem],
        out_specs=vmem,
        scratch_shapes=[pltpu.SemaphoreType.DMA, pltpu.SemaphoreType.DMA, pltpu.SemaphoreType.DMA],
        compiler_params=pltpu.CompilerParams(collective_id=1, has_side_effects=True),
    )(amplifiers)
    flat = pl.pallas_call(
        crosstalk_kernel,
        out_shape=jax.ShapeDtypeStruct((4096, 128), jnp.float32),
        in_specs=[vmem, vmem],
        out_specs=vmem,
    )(got, mix)
    flat = flat.reshape(32, 16, 4, 2, 128)
    return jnp.transpose(flat, (0, 1, 3, 2, 4)).reshape(32, 16, 1, 2, 512)


def solution(mesh):
    placed = (
        P(("sensor", "rows"), None, None, None),
        P(("sensor", "rows"), None, None),
        P(("sensor", "rows"), None),
        P(),
        P(),
        P(),
    )
    return jax.shard_map(
        shards,
        mesh=mesh,
        in_specs=placed,
        out_specs=P(None, None, "rows", "sensor", None),
        check_vma=False,
    )
```
